512 devices in a mesh: station: 32 (over y, x), tm: 16 (over z, core).
Axes of the slice: x: 4, y: 8, z: 8, core: 2. Of those that a mesh axis runs over, the one named last changes fastest.
Arguments:
- spectra: bfloat16 [16, 128, 4096], P('tm', 'station'), may hold values from -5 to 5
- valid: int32 [16, 128], P('tm', 'station'), may hold values from 0 to 1, as said below
- pair_blocks: int32 [32, 17], P('station'), may hold values from 0 to 31, as said below
Outputs:
- correlations: float32 [8704, 512], P(('station', 'tm'))
The draws below stay inside these ranges and needn't reach their ends.
Inputs may be any that keep to these rules, and one draw needn't show every extreme that they name: `pair_blocks`: row d begins with d, its 17 entries are distinct, and every unordered pair of blocks appears in some row. `valid`: each station misses one cyclic run of 1 to 7 hours.
All inputs are finite; a program needn't handle non-finite values.
Results may differ from the reference program's by a relative error of at most 0.0026.
Values may be sent and summed in bfloat16 or wider, within the bound.
A program may use at most 64 MiB of HBM per device.

```python
import math
import jax
import jax.numpy as jnp
from jax import lax

SB = 4
HR_DEV = 1
F = 2048
LAGS = 512
STATIONS = 128
HOURS = 16
SLOTS = 17
PAIR_ROWS = 8704
N_STATION = 32


def draw_pair_blocks(key, part):
    order = jax.random.permutation(jax.random.fold_in(key, 11), N_STATION)
    ranks = jnp.argsort(order)
    steps_ahead = jnp.arange(SLOTS, dtype=jnp.int32)
    where_at = (ranks[:, None] + steps_ahead[None, :]) % N_STATION
    return order[where_at].astype(jnp.int32)


def draw_valid(key, part):
    begin_key = jax.random.fold_in(key, 21)
    length_key = jax.random.fold_in(key, 22)
    begins = jax.random.randint(begin_key, (STATIONS,), 0, HOURS)
    lengths = jax.random.randint(length_key, (STATIONS,), 1, HOURS // 2)
    hour_ids = jnp.arange(HOURS, dtype=jnp.int32)[:, None]
    in_gap = (hour_ids - begins[None, :]) % HOURS < lengths[None, :]
    return jnp.where(in_gap, 0, 1).astype(jnp.int32)


def levels(stream_key, dims, cuts, least, largest):
    def one(position, shards_of):
        draws = jax.random.uniform(jax.random.fold_in(jax.random.fold_in(stream_key, 6), position), (shards_of,), jnp.float32, least / len(cuts), largest / len(cuts))
        return jnp.repeat(jnp.exp(draws), dims[position] // shards_of).reshape((-1,) + (1,) * (len(dims) - position - 1))

    gain = one(*cuts[0])
    for cut in cuts[1:]:
        gain = gain * one(*cut)
    return gain


def gaussian(own_key, shape, width, limit, shards=(), held_as=jnp.bfloat16):
    array = jax.random.normal(own_key, shape, jnp.float32) * width
    if len(shards) > 0:
        array = levels(own_key, shape, shards, -0.22, 0.18) * array
    return jnp.clip(array, min=-limit, max=limit).astype(held_as)


def setup_inputs(seed: int = 0) -> dict:
    streams_of = jax.random.split(jax.random.key(seed), 4)
    return {
        "spectra": gaussian(streams_of[0], (HOURS, STATIONS, 2 * F), 0.7, 5.0, ((0, 16), (1, 32))),
        "valid": draw_valid(jax.random.fold_in(streams_of[3], 71), 0),
        "pair_blocks": draw_pair_blocks(jax.random.fold_in(streams_of[3], 71), 0),
    }


def make_lag_table(half_width, lag_count):
    bins = jnp.arange(half_width, dtype=jnp.int32)
    shifts = jnp.arange(lag_count, dtype=jnp.int32) - lag_count // 2
    phase = (2 * bins[:, None] + 1) * shifts[None, :] % (4 * half_width)
    angle = phase.astype(jnp.float32) * (math.pi / (2.0 * half_width))
    return jnp.concatenate([jnp.cos(angle), -jnp.sin(angle)], axis=0).astype(jnp.bfloat16)

def reference(spectra, valid, pair_blocks):
    groups = HOURS // HR_DEV
    masked = spectra * valid[:, :, None].astype(jnp.bfloat16)
    blocks = masked.reshape(HOURS, N_STATION, SB, 2 * F).transpose(1, 0, 2, 3)
    flags = valid.astype(jnp.float32).reshape(HOURS, N_STATION, SB).transpose(1, 0, 2)
    lag_table = make_lag_table(F, LAGS).astype(jnp.float32)
    lag_scale = 4.0 / math.sqrt(F)

    def one_owner(owner):
        own_block = blocks[owner].astype(jnp.float32).reshape(groups, HR_DEV, SB, 2 * F)
        partners = blocks[pair_blocks[owner]].astype(jnp.float32).reshape(SLOTS, groups, HR_DEV, SB, 2 * F)
        own_real, own_imag = (own_block[..., :F], own_block[..., F:])
        part_real, part_imag = (partners[..., :F], partners[..., F:])
        cross_real = jnp.einsum('ghaf,kghbf->kgabf', own_real, part_real) + jnp.einsum('ghaf,kghbf->kgabf', own_imag, part_imag)
        cross_imag = jnp.einsum('ghaf,kghbf->kgabf', own_imag, part_real) - jnp.einsum('ghaf,kghbf->kgabf', own_real, part_imag)
        stacked = jnp.concatenate([cross_real, cross_imag], axis=-1).astype(jnp.bfloat16)
        stacked = lax.optimization_barrier(stacked)
        summed = lax.optimization_barrier(jnp.sum(stacked.astype(jnp.float32), axis=1)).reshape(SLOTS * SB * SB, 2 * F)
        lagged = jnp.dot(summed, lag_table, precision=lax.Precision.HIGHEST)
        own_flags = flags[owner]
        part_flags = flags[pair_blocks[owner]]
        counts = jnp.einsum('ha,khb->kab', own_flags, part_flags).reshape(SLOTS * SB * SB)
        return lagged * lag_scale / counts[:, None]
    owners = jnp.arange(N_STATION, dtype=jnp.int32)
    result = lax.map(one_owner, owners)
    return result.reshape(PAIR_ROWS, LAGS)
```

```python
import math

import jax
import jax.numpy as jnp
import numpy as np
from jax import lax
from jax.experimental import pallas as pl
from jax.experimental.pallas import tpu as pltpu
from jax.sharding import PartitionSpec as P

LAGS = 512
NX, NY = 4, 8
NT = 16
SLOTS = 17
ROWS = 17
HALF = 2048
BINS = HALF // NT
TILES = 17
CUT = 9
f32, bf16 = jnp.float32, jnp.bfloat16


def lag_table():
    bins = np.arange(HALF, dtype=np.int64)
    shifts = np.arange(LAGS, dtype=np.int64) - LAGS // 2
    phase = (2 * bins[:, None] + 1) * shifts[None, :] % (4 * HALF)
    angle = phase * (math.pi / (2.0 * HALF))
    table = np.stack([np.cos(angle), -np.sin(angle)]).reshape(2, NT, BINS, LAGS)
    return table.transpose(1, 0, 2, 3).reshape(NT, 2 * BINS, LAGS).astype(bf16)


def kernel(plan, valid, x_ref, table_ref, out_ref,
           msg, got, G, own, stack, recv, tab, pairs,
           tab_sem, s1, r1, say, ray, sax, rax, sbx, rbx, sby, rby, s4, r4):
    st, t = lax.axis_index("station"), lax.axis_index("tm")
    y, x = st // NX, st % NX

    def plane(yy, xx):
        return {"station": (yy % NY) * NX + xx % NX}

    barrier = pltpu.get_barrier_semaphore()
    for j in range(1, NT):
        pl.semaphore_signal(barrier, inc=1, device_id={"tm": (t + j) % NT},
                            device_id_type=pl.DeviceIdType.MESH)
    for j in range(1, NX):
        pl.semaphore_signal(barrier, inc=1, device_id=plane(y, x + j),
                            device_id_type=pl.DeviceIdType.MESH)
    for j in (1, NY - 1):
        pl.semaphore_signal(barrier, inc=1, device_id=plane(y + j, x),
                            device_id_type=pl.DeviceIdType.MESH)

    tab_copy = pltpu.make_async_copy(table_ref, tab, tab_sem)
    tab_copy.start()

    row = lax.broadcasted_iota(jnp.int32, (4, BINS), 0)
    flag = jnp.where(row == 0, valid[0, 0],
                     jnp.where(row == 1, valid[0, 1],
                               jnp.where(row == 2, valid[0, 2], valid[0, 3]))).astype(f32)
    for j in range(NT):
        re = x_ref[0, :, j * BINS:(j + 1) * BINS].astype(f32) * flag
        im = x_ref[0, :, HALF + j * BINS:HALF + (j + 1) * BINS].astype(f32) * flag
        msg[j] = jnp.concatenate([re, im, flag, flag], axis=0).astype(bf16)

    pl.semaphore_wait(barrier, NT - 1 + NX - 1 + 2)

    first = []
    for j in range(1, NT):
        c = pltpu.make_async_remote_copy(
            src_ref=msg.at[(t + j) % NT], dst_ref=got.at[t], send_sem=s1.at[j], recv_sem=r1.at[j],
            device_id={"tm": (t + j) % NT}, device_id_type=pl.DeviceIdType.MESH)
        c.start()
        first.append(c)
    got[t] = msg[t]
    for c in first:
        c.wait_recv()
    lane = lax.broadcasted_iota(jnp.int32, (8, BINS), 1)
    flags = jnp.zeros((8, BINS), f32)
    for h in range(NT):
        tile = got[h].astype(f32)
        G[y, x, h + (1 if h >= CUT - 1 else 0)] = tile[0:8].astype(bf16)
        flags = jnp.where(lane == h, tile[8:16], flags)
        for q in range(8):
            own[h, q] = jnp.broadcast_to(tile[q:q + 1], (8, BINS))
    G[y, x, CUT - 1] = flags.astype(bf16)

    sends = []

    def send(ref, to, ssem, rsem):
        c = pltpu.make_async_remote_copy(src_ref=ref, dst_ref=ref, send_sem=ssem, recv_sem=rsem,
                                         device_id=to, device_id_type=pl.DeviceIdType.MESH)
        c.start()
        sends.append(c)
        return c

    def A(yy, xx):
        return G.at[yy % NY, xx % NX, pl.ds(0, CUT)]

    def B(yy, xx):
        return G.at[yy % NY, xx % NX, pl.ds(CUT, TILES - CUT)]

    def BY(yy):
        return G.at[yy % NY, :, pl.ds(CUT, TILES - CUT)]

    def send_ax(n, yy):
        return [send(A(yy, x), plane(y, x + j), sax.at[n, j], rax.at[n, j]) for j in range(1, NX)]

    bx = [send(B(y, x), plane(y, x + j), sbx.at[j], rbx.at[j]) for j in range(1, NX)]
    up = send(A(y, x), plane(y + 1, x), say.at[0, 0], ray.at[0, 0])
    down = send(A(y, x), plane(y - 1, x), say.at[1, 0], ray.at[1, 0])
    ax = send_ax(0, y)
    for c in bx:
        c.wait_recv()
    bup = send(BY(y), plane(y + 1, x), sby.at[0, 0], rby.at[0, 0])
    bdown = send(BY(y), plane(y - 1, x), sby.at[1, 0], rby.at[1, 0])
    for s in range(1, 5):
        up.wait_recv()
        if s < 4:
            down.wait_recv()
            up = send(A(y - s, x), plane(y + 1, x), say.at[0, s], ray.at[0, s])
            if s < 3:
                down = send(A(y + s, x), plane(y - 1, x), say.at[1, s], ray.at[1, s])
        ax += send_ax(2 * s - 1, y - s)
        if s < 4:
            ax += send_ax(2 * s, y + s)
        bdown.wait_recv()
        if s < 4:
            bup.wait_recv()
            bdown = send(BY(y + s), plane(y - 1, x), sby.at[1, s], rby.at[1, s])
            if s < 3:
                bup = send(BY(y - s), plane(y + 1, x), sby.at[0, s], rby.at[0, s])
    for c in ax:
        c.wait_recv()

    top = lax.broadcasted_iota(jnp.int32, (8, BINS), 0) < 4

    def slots(ks):
        tiles = []
        for k in ks:
            blk = plan[0, k]
            tiles.append((blk // NX, blk % NX))
        acc = [[[None, None] for _ in range(4)] for _ in ks]
        for h in range(NT):
            g = [G[by, bx_, h + (1 if h >= CUT - 1 else 0)].astype(f32) for by, bx_ in tiles]
            for a in range(4):
                for c in range(2):
                    o = own[h, 4 * c + a]
                    for n in range(len(ks)):
                        p = o * g[n]
                        acc[n][a][c] = p if h == 0 else acc[n][a][c] + p
        for n, k in enumerate(ks):
            for half in range(2):
                (e1, e2), (o1, o2) = acc[n][2 * half], acc[n][2 * half + 1]
                roll = lambda v: pltpu.roll(v, 4, 0)
                re = jnp.where(top, e1 + roll(e2), roll(o1) + o2)
                im = jnp.where(top, e2 - roll(e1), roll(o2) - o1)
                stack[2 * k + half, :, 0:BINS] = re.astype(bf16)
                stack[2 * k + half, :, BINS:2 * BINS] = im.astype(bf16)
            by, bx_ = tiles[n]
            fl = G[by, bx_, CUT - 1].astype(f32)
            of = G[y, x, CUT - 1].astype(f32)
            fe = jnp.where(top, fl, pltpu.roll(fl, 4, 0))
            for half in range(2):
                oa = jnp.where(top, jnp.broadcast_to(of[2 * half:2 * half + 1], (8, BINS)),
                               jnp.broadcast_to(of[2 * half + 1:2 * half + 2], (8, BINS)))
                pairs[2 * k + half] = fe * oa

    slots([0])

    def two(i, carry):
        slots([2 * i + 1, 2 * i + 2])
        return carry

    lax.fori_loop(0, 8, two, 0)

    last = []
    for j in range(1, NT):
        to = (t + j) % NT
        c = pltpu.make_async_remote_copy(
            src_ref=stack.at[pl.ds(ROWS * to // 8, 3)], dst_ref=recv.at[t],
            send_sem=s4.at[j], recv_sem=r4.at[j],
            device_id={"tm": to}, device_id_type=pl.DeviceIdType.MESH)
        c.start()
        last.append(c)
    base = ROWS * t // 8
    mine = jnp.concatenate([stack[base + i].astype(f32) for i in range(3)], axis=0).astype(bf16)
    counts = jnp.concatenate(
        [jnp.sum(pairs[base + i], axis=1, keepdims=True) for i in range(3)], axis=0)
    tab_copy.wait()
    acc = jnp.dot(mine, tab[t], preferred_element_type=f32)
    for j in range(1, NT):
        last[j - 1].wait_recv()
        src = (t + NT - j) % NT
        lhs = jnp.concatenate([recv[src, i].astype(f32) for i in range(3)], axis=0).astype(bf16)
        acc = acc + jnp.dot(lhs, tab[src], preferred_element_type=f32)
    res = acc * (4.0 / math.sqrt(HALF)) / counts
    shift = ROWS * t % 8
    res = pltpu.roll(res, (24 - shift) % 24, 0)
    out_ref[...] = res[0:ROWS]
    for c in first + sends + last:
        c.wait_send()


def per_device(spectra, valid, pair_blocks):
    dma = pltpu.SemaphoreType.DMA
    vmem = pl.BlockSpec(memory_space=pltpu.VMEM)
    smem = pl.BlockSpec(memory_space=pltpu.SMEM)
    return pl.pallas_call(
        kernel,
        out_shape=jax.ShapeDtypeStruct((ROWS, LAGS), f32),
        in_specs=[smem, smem, vmem, pl.BlockSpec(memory_space=pl.ANY)],
        out_specs=vmem,
        scratch_shapes=[
            pltpu.VMEM((NT, 16, BINS), bf16),
            pltpu.VMEM((NT, 16, BINS), bf16),
            pltpu.VMEM((NY, NX, TILES, 8, BINS), bf16),
            pltpu.VMEM((NT, 8, 8, BINS), f32),
            pltpu.VMEM((2 * SLOTS, 8, 2 * BINS), bf16),
            pltpu.VMEM((NT, 3, 8, 2 * BINS), bf16),
            pltpu.VMEM((NT, 2 * BINS, LAGS), bf16),
            pltpu.VMEM((2 * SLOTS, 8, BINS), f32),
            dma, dma((NT,)), dma((NT,)), dma((2, 4)), dma((2, 4)),
            dma((NY, NX)), dma((NY, NX)), dma((NX,)), dma((NX,)),
            dma((2, 4)), dma((2, 4)), dma((NT,)), dma((NT,)),
        ],
        compiler_params=pltpu.CompilerParams(
            collective_id=0, has_side_effects=True, vmem_limit_bytes=24 << 20),
    )(pair_blocks, valid, spectra, jnp.asarray(lag_table()))


def solution(mesh):
    placed = (P("tm", "station", None), P("tm", "station"), P("station", None))
    return jax.shard_map(
        per_device,
        mesh=mesh,
        in_specs=placed,
        out_specs=P(("station", "tm"), None),
        check_vma=False,
    )
```

```python
import math

import jax
import jax.numpy as jnp
import numpy as np
from jax import lax
from jax.experimental import pallas as pl
from jax.experimental.pallas import tpu as pltpu
from jax.sharding import PartitionSpec as P

LAGS = 512
NX, NY = 4, 8
NT = 16
SLOTS = 17
ROWS = 17
HALF = 2048
BINS = HALF // NT
TILES = 17
CUT = 9
f32, bf16 = jnp.float32, jnp.bfloat16


def lag_base():
    shifts = np.arange(LAGS, dtype=np.int64) - LAGS // 2
    unit = math.pi / (2.0 * HALF)

    def both(steps):
        angle = steps[:, None] * shifts[None, :] % (4 * HALF) * unit
        return np.stack([np.cos(angle), np.sin(angle)]).astype(np.float32)

    base = both(2 * np.arange(BINS, dtype=np.int64) + 1)
    turn = both(2 * BINS * np.arange(NT, dtype=np.int64))
    return base, turn


def kernel(plan_ref, valid_ref, spectra_ref, base_ref, turn_ref, out_ref,
           plan, valid, x_ref, base, turn, msg, got, G, own, stack, recv, tab, pairs,
           in_sem, s1, r1, say, ray, sax, rax, sbx, rbx, sby, rby, s4, r4):
    st, t = lax.axis_index("station"), lax.axis_index("tm")
    y, x = st // NX, st % NX

    def plane(yy, xx):
        return {"station": (yy % NY) * NX + xx % NX}

    loads = [pltpu.make_async_copy(a, b, in_sem.at[i]) for i, (a, b) in enumerate(
        [(spectra_ref, x_ref), (valid_ref, valid), (plan_ref, plan), (base_ref, base),
         (turn_ref, turn)])]
    for c in loads:
        c.start()

    barrier = pltpu.get_barrier_semaphore()
    for j in range(1, NT):
        pl.semaphore_signal(barrier, inc=1, device_id={"tm": (t + j) % NT},
                            device_id_type=pl.DeviceIdType.MESH)
    for j in range(1, NX):
        pl.semaphore_signal(barrier, inc=1, device_id=plane(y, x + j),
                            device_id_type=pl.DeviceIdType.MESH)
    for j in (1, NY - 1):
        pl.semaphore_signal(barrier, inc=1, device_id=plane(y + j, x),
                            device_id_type=pl.DeviceIdType.MESH)

    loads[0].wait()
    loads[1].wait()
    row = lax.broadcasted_iota(jnp.int32, (4, BINS), 0)
    flag = jnp.where(row == 0, valid[0, 0],
                     jnp.where(row == 1, valid[0, 1],
                               jnp.where(row == 2, valid[0, 2], valid[0, 3]))).astype(f32)
    for j in range(NT):
        re = x_ref[0, :, j * BINS:(j + 1) * BINS].astype(f32) * flag
        im = x_ref[0, :, HALF + j * BINS:HALF + (j + 1) * BINS].astype(f32) * flag
        msg[j] = jnp.concatenate([re, im, flag, flag], axis=0).astype(bf16)

    pl.semaphore_wait(barrier, NT - 1 + NX - 1 + 2)

    first = []
    for j in range(1, NT):
        c = pltpu.make_async_remote_copy(
            src_ref=msg.at[(t + j) % NT], dst_ref=got.at[t], send_sem=s1.at[j], recv_sem=r1.at[j],
            device_id={"tm": (t + j) % NT}, device_id_type=pl.DeviceIdType.MESH)
        c.start()
        first.append(c)
    got[t] = msg[t]

    for c in loads[2:]:
        c.wait()

    def fill(j, carry):
        tc = turn[0, pl.ds(j, 1), :]
        ts = turn[1, pl.ds(j, 1), :]
        for i in range(0, BINS, 16):
            bc, bs = base[0, i:i + 16], base[1, i:i + 16]
            tab[j, i:i + 16] = (bc * tc - bs * ts).astype(bf16)
            tab[j, BINS + i:BINS + i + 16] = (-(bs * tc + bc * ts)).astype(bf16)
        return carry

    lax.fori_loop(0, NT, fill, 0)
    for c in first:
        c.wait_recv()
    lane = lax.broadcasted_iota(jnp.int32, (8, BINS), 1)
    flags = jnp.zeros((8, BINS), f32)
    for h in range(NT):
        tile = got[h].astype(f32)
        G[y, x, h + (1 if h >= CUT - 1 else 0)] = tile[0:8].astype(bf16)
        flags = jnp.where(lane == h, tile[8:16], flags)
        for q in range(8):
            own[h, q] = jnp.broadcast_to(tile[q:q + 1], (8, BINS))
    G[y, x, CUT - 1] = flags.astype(bf16)

    sends = []

    def send(ref, to, ssem, rsem):
        c = pltpu.make_async_remote_copy(src_ref=ref, dst_ref=ref, send_sem=ssem, recv_sem=rsem,
                                         device_id=to, device_id_type=pl.DeviceIdType.MESH)
        c.start()
        sends.append(c)
        return c

    def A(yy, xx):
        return G.at[yy % NY, xx % NX, pl.ds(0, CUT)]

    def B(yy, xx):
        return G.at[yy % NY, xx % NX, pl.ds(CUT, TILES - CUT)]

    def BY(yy):
        return G.at[yy % NY, :, pl.ds(CUT, TILES - CUT)]

    def send_ax(n, yy):
        return [send(A(yy, x), plane(y, x + j), sax.at[n, j], rax.at[n, j]) for j in range(1, NX)]

    bx = [send(B(y, x), plane(y, x + j), sbx.at[j], rbx.at[j]) for j in range(1, NX)]
    up = send(A(y, x), plane(y + 1, x), say.at[0, 0], ray.at[0, 0])
    down = send(A(y, x), plane(y - 1, x), say.at[1, 0], ray.at[1, 0])
    ax = send_ax(0, y)
    for c in bx:
        c.wait_recv()
    bup = send(BY(y), plane(y + 1, x), sby.at[0, 0], rby.at[0, 0])
    bdown = send(BY(y), plane(y - 1, x), sby.at[1, 0], rby.at[1, 0])
    for s in range(1, 5):
        up.wait_recv()
        if s < 4:
            down.wait_recv()
            up = send(A(y - s, x), plane(y + 1, x), say.at[0, s], ray.at[0, s])
            if s < 3:
                down = send(A(y + s, x), plane(y - 1, x), say.at[1, s], ray.at[1, s])
        ax += send_ax(2 * s - 1, y - s)
        if s < 4:
            ax += send_ax(2 * s, y + s)
        bdown.wait_recv()
        if s < 4:
            bup.wait_recv()
            bdown = send(BY(y + s), plane(y - 1, x), sby.at[1, s], rby.at[1, s])
            if s < 3:
                bup = send(BY(y - s), plane(y + 1, x), sby.at[0, s], rby.at[0, s])
    for c in ax:
        c.wait_recv()

    top = lax.broadcasted_iota(jnp.int32, (8, BINS), 0) < 4

    def slots(ks):
        tiles = []
        for k in ks:
            blk = plan[0, k]
            tiles.append((blk // NX, blk % NX))
        acc = [[[None, None] for _ in range(4)] for _ in ks]
        for h in range(NT):
            g = [G[by, bx_, h + (1 if h >= CUT - 1 else 0)].astype(f32) for by, bx_ in tiles]
            for a in range(4):
                for c in range(2):
                    o = own[h, 4 * c + a]
                    for n in range(len(ks)):
                        p = o * g[n]
                        acc[n][a][c] = p if h == 0 else acc[n][a][c] + p
        for n, k in enumerate(ks):
            for half in range(2):
                (e1, e2), (o1, o2) = acc[n][2 * half], acc[n][2 * half + 1]
                roll = lambda v: pltpu.roll(v, 4, 0)
                re = jnp.where(top, e1 + roll(e2), roll(o1) + o2)
                im = jnp.where(top, e2 - roll(e1), roll(o2) - o1)
                stack[2 * k + half, :, 0:BINS] = re.astype(bf16)
                stack[2 * k + half, :, BINS:2 * BINS] = im.astype(bf16)
            by, bx_ = tiles[n]
            fl = G[by, bx_, CUT - 1].astype(f32)
            of = G[y, x, CUT - 1].astype(f32)
            fe = jnp.where(top, fl, pltpu.roll(fl, 4, 0))
            for half in range(2):
                oa = jnp.where(top, jnp.broadcast_to(of[2 * half:2 * half + 1], (8, BINS)),
                               jnp.broadcast_to(of[2 * half + 1:2 * half + 2], (8, BINS)))
                pairs[2 * k + half] = fe * oa

    slots([0])

    def two(i, carry):
        slots([2 * i + 1, 2 * i + 2])
        return carry

    lax.fori_loop(0, 8, two, 0)

    last = []
    for j in range(1, NT):
        to = (t + j) % NT
        c = pltpu.make_async_remote_copy(
            src_ref=stack.at[pl.ds(ROWS * to // 8, 3)], dst_ref=recv.at[t],
            send_sem=s4.at[j], recv_sem=r4.at[j],
            device_id={"tm": to}, device_id_type=pl.DeviceIdType.MESH)
        c.start()
        last.append(c)
    base = ROWS * t // 8
    mine = jnp.concatenate([stack[base + i].astype(f32) for i in range(3)], axis=0).astype(bf16)
    counts = jnp.concatenate(
        [jnp.sum(pairs[base + i], axis=1, keepdims=True) for i in range(3)], axis=0)
    acc = jnp.dot(mine, tab[t], preferred_element_type=f32)
    for j in range(1, NT):
        last[j - 1].wait_recv()
        src = (t + NT - j) % NT
        lhs = jnp.concatenate([recv[src, i].astype(f32) for i in range(3)], axis=0).astype(bf16)
        acc = acc + jnp.dot(lhs, tab[src], preferred_element_type=f32)
    res = acc * (4.0 / math.sqrt(HALF)) / counts
    shift = ROWS * t % 8
    res = pltpu.roll(res, (24 - shift) % 24, 0)
    out_ref[...] = res[0:ROWS]
    for c in first + sends + last:
        c.wait_send()


def per_device(spectra, valid, pair_blocks):
    dma = pltpu.SemaphoreType.DMA
    anywhere = pl.BlockSpec(memory_space=pl.ANY)
    base, turn = lag_base()
    return pl.pallas_call(
        kernel,
        out_shape=jax.ShapeDtypeStruct((ROWS, LAGS), f32),
        in_specs=[anywhere] * 5,
        out_specs=pl.BlockSpec(memory_space=pltpu.VMEM),
        scratch_shapes=[
            pltpu.SMEM((1, SLOTS), jnp.int32),
            pltpu.SMEM((1, 4), jnp.int32),
            pltpu.VMEM((1, 4, 2 * HALF), bf16),
            pltpu.VMEM((2, BINS, LAGS), f32),
            pltpu.VMEM((2, NT, LAGS), f32),
            pltpu.VMEM((NT, 16, BINS), bf16),
            pltpu.VMEM((NT, 16, BINS), bf16),
            pltpu.VMEM((NY, NX, TILES, 8, BINS), bf16),
            pltpu.VMEM((NT, 8, 8, BINS), f32),
            pltpu.VMEM((2 * SLOTS, 8, 2 * BINS), bf16),
            pltpu.VMEM((NT, 3, 8, 2 * BINS), bf16),
            pltpu.VMEM((NT, 2 * BINS, LAGS), bf16),
            pltpu.VMEM((2 * SLOTS, 8, BINS), f32),
            dma((5,)), dma((NT,)), dma((NT,)), dma((2, 4)), dma((2, 4)),
            dma((NY, NX)), dma((NY, NX)), dma((NX,)), dma((NX,)),
            dma((2, 4)), dma((2, 4)), dma((NT,)), dma((NT,)),
        ],
        compiler_params=pltpu.CompilerParams(
            collective_id=0, has_side_effects=True, vmem_limit_bytes=60 << 20),
    )(pair_blocks, valid, spectra, jnp.asarray(base), jnp.asarray(turn))


def solution(mesh):
    placed = (P("tm", "station", None), P("tm", "station"), P("station", None))
    return jax.shard_map(
        per_device,
        mesh=mesh,
        in_specs=placed,
        out_specs=P(("station", "tm"), None),
        check_vma=False,
    )
```

```python
import math

import jax
import jax.numpy as jnp
import numpy as np
from jax import lax
from jax.experimental import pallas as pl
from jax.experimental.pallas import tpu as pltpu
from jax.sharding import PartitionSpec as P

LAGS = 512
NX, NY = 4, 8
NT = 16
SLOTS = 17
ROWS = 17
HALF = 2048
BINS = HALF // NT
TILES = 17
CUT = 12
DIST = (0, 1, 7, 2, 6, 3, 5, 4)
PEERS = [(dz, dc) for dz in DIST for dc in (0, 1)][1:]
HOP = (1, NY - 1, 2, NY - 2, 1, NY - 1, 2, NY - 2)
f32, bf16 = jnp.float32, jnp.bfloat16


def lag_base():
    shifts = np.arange(LAGS, dtype=np.int64) - LAGS // 2
    unit = math.pi / (2.0 * HALF)

    def both(steps):
        angle = steps[:, None] * shifts[None, :] % (4 * HALF) * unit
        return np.stack([np.cos(angle), np.sin(angle)]).astype(np.float32)

    base = both(2 * np.arange(BINS, dtype=np.int64) + 1)
    turn = both(2 * BINS * np.arange(NT, dtype=np.int64))
    return base, turn


def kernel(plan_ref, valid_ref, spectra_ref, base_ref, turn_ref, out_ref,
           plan, valid, x_ref, base, turn, msg, got, G, own, stack, recv, tab, pairs,
           in_sem, s1, r1, say, ray, sax, rax, sbx, rbx, sby, rby, s4, r4):
    st, t = lax.axis_index("station"), lax.axis_index("tm")
    y, x = st // NX, st % NX
    z, core = t // 2, t % 2

    def line(dz, dc):
        return (z + dz) % 8 * 2 + (core + dc) % 2

    def slot(dz, dc):
        return 2 * DIST.index(dz % 8) + dc

    def tile(n):
        return n if n < CUT else n + 1

    def plane(yy, xx):
        return {"station": (yy % NY) * NX + xx % NX}

    loads = [pltpu.make_async_copy(a, b, in_sem.at[i]) for i, (a, b) in enumerate(
        [(spectra_ref, x_ref), (valid_ref, valid), (plan_ref, plan), (base_ref, base),
         (turn_ref, turn)])]
    for c in loads:
        c.start()

    barrier = pltpu.get_barrier_semaphore()
    for p in reversed(PEERS):
        pl.semaphore_signal(barrier, inc=1, device_id={"tm": line(*p)},
                            device_id_type=pl.DeviceIdType.MESH)
    for j in range(1, NX):
        pl.semaphore_signal(barrier, inc=1, device_id=plane(y, x + j),
                            device_id_type=pl.DeviceIdType.MESH)
    for j in (1, 2, NY - 2, NY - 1):
        pl.semaphore_signal(barrier, inc=1, device_id=plane(y + j, x),
                            device_id_type=pl.DeviceIdType.MESH)

    loads[0].wait()
    loads[1].wait()
    row = lax.broadcasted_iota(jnp.int32, (4, BINS), 0)
    flag = jnp.where(row == 0, valid[0, 0],
                     jnp.where(row == 1, valid[0, 1],
                               jnp.where(row == 2, valid[0, 2], valid[0, 3]))).astype(f32)
    for j in range(NT):
        re = x_ref[0, :, j * BINS:(j + 1) * BINS].astype(f32) * flag
        im = x_ref[0, :, HALF + j * BINS:HALF + (j + 1) * BINS].astype(f32) * flag
        msg[j] = jnp.concatenate([re, im, flag, flag], axis=0).astype(bf16)

    pl.semaphore_wait(barrier, NT - 1 + NX - 1 + 4)

    first = {}
    for dz, dc in reversed(PEERS):
        to = line(dz, dc)
        c = pltpu.make_async_remote_copy(
            src_ref=msg.at[to], dst_ref=got.at[slot(-dz, dc)], send_sem=s1.at[slot(-dz, dc)],
            recv_sem=r1.at[slot(-dz, dc)], device_id={"tm": to},
            device_id_type=pl.DeviceIdType.MESH)
        c.start()
        first[slot(-dz, dc)] = c
    got[0] = msg[t]

    for c in loads[2:]:
        c.wait()

    def fill(j, carry):
        tc = turn[0, pl.ds(j, 1), :]
        ts = turn[1, pl.ds(j, 1), :]
        for i in range(0, BINS, 16):
            bc, bs = base[0, i:i + 16], base[1, i:i + 16]
            tab[j, i:i + 16] = (bc * tc - bs * ts).astype(bf16)
            tab[j, BINS + i:BINS + i + 16] = (-(bs * tc + bc * ts)).astype(bf16)
        return carry

    lax.fori_loop(0, NT, fill, 0)
    sends = []

    def send(ref, to, ssem, rsem):
        c = pltpu.make_async_remote_copy(src_ref=ref, dst_ref=ref, send_sem=ssem, recv_sem=rsem,
                                         device_id=to, device_id_type=pl.DeviceIdType.MESH)
        c.start()
        sends.append(c)
        return c

    def A(yy, xx):
        return G.at[yy % NY, xx % NX, pl.ds(0, CUT)]

    def B(yy, xx):
        return G.at[yy % NY, xx % NX, pl.ds(CUT, TILES - CUT)]

    def BY(yy):
        return G.at[yy % NY, :, pl.ds(CUT, TILES - CUT)]

    def send_ax(n, yy):
        return [send(A(yy, x), plane(y, x + j), sax.at[n, j], rax.at[n, j]) for j in range(1, NX)]

    def far(block, n, ssem, rsem):
        return send(block, plane(y + HOP[n], x), ssem.at[n], rsem.at[n])

    def relay(block, half, ssem, rsem):
        return [far(block(y - 2), 4, ssem, rsem), far(block(y + 2), 5, ssem, rsem),
                far(half(y - 2, 0), 6, ssem, rsem), far(half(y + 2, 1), 7, ssem, rsem)]

    def A_half(yy, h):
        return G.at[yy % NY, x, pl.ds(h * (CUT // 2), CUT // 2 if h == 0 else CUT - CUT // 2)]

    def B_half(yy, h):
        n = TILES - CUT
        return G.at[yy % NY, :, pl.ds(CUT + h * (n // 2), n // 2 if h == 0 else n - n // 2)]

    def arrive(n):
        if n > 0:
            first[n].wait_recv()
        G[y, x, tile(n)] = got[n, 0:8]

    for n in range(CUT):
        arrive(n)
    ay = [far(A(y, x), n, say, ray) for n in (0, 1, 2, 3)]
    for n in range(CUT, NT):
        arrive(n)
    lane = lax.broadcasted_iota(jnp.int32, (8, BINS), 1)
    flags = jnp.zeros((8, BINS), f32)
    for n in range(NT):
        flags = jnp.where(lane == n, got[n, 8:16].astype(f32), flags)
    G[y, x, CUT] = flags.astype(bf16)
    bx = [send(B(y, x), plane(y, x + j), sbx.at[j], rbx.at[j]) for j in range(1, NX)]
    ax = send_ax(0, y)
    for n in range(NT):
        mine = got[n, 0:8].astype(f32)
        for q in range(8):
            own[n, q] = jnp.broadcast_to(mine[q:q + 1], (8, BINS))
    for c in bx:
        c.wait_recv()
    by = [far(BY(y), n, sby, rby) for n in range(4)]
    ay[2].wait_recv()
    ay[3].wait_recv()
    ay += relay(lambda yy: A(yy, x), A_half, say, ray)
    ay[0].wait_recv()
    ax += send_ax(1, y - 1)
    ay[1].wait_recv()
    ax += send_ax(2, y + 1)
    ax += send_ax(3, y - 2)
    ax += send_ax(4, y + 2)
    by[2].wait_recv()
    by[3].wait_recv()
    by += relay(BY, B_half, sby, rby)
    ay[4].wait_recv()
    ax += send_ax(5, y - 3)
    ay[5].wait_recv()
    ax += send_ax(6, y + 3)
    ay[6].wait_recv()
    ay[7].wait_recv()
    ax += send_ax(7, y + 4)
    for c in by[:2] + by[4:] + ax:
        c.wait_recv()

    top = lax.broadcasted_iota(jnp.int32, (8, BINS), 0) < 4

    def slots(ks):
        tiles = []
        for k in ks:
            blk = plan[0, k]
            tiles.append((blk // NX, blk % NX))
        acc = [[[None, None] for _ in range(4)] for _ in ks]
        for h in range(NT):
            g = [G[by, bx_, tile(h)].astype(f32) for by, bx_ in tiles]
            for a in range(4):
                for c in range(2):
                    o = own[h, 4 * c + a]
                    for n in range(len(ks)):
                        p = o * g[n]
                        acc[n][a][c] = p if h == 0 else acc[n][a][c] + p
        for n, k in enumerate(ks):
            for a in range(4):
                p, q = acc[n][a]
                re = p + pltpu.roll(q, 4, 0)
                im = q - pltpu.roll(p, 4, 0)
                stack[4 * k + a, :, 0:BINS] = re[0:4].astype(bf16)
                stack[4 * k + a, :, BINS:2 * BINS] = im[0:4].astype(bf16)
            by, bx_ = tiles[n]
            fl = G[by, bx_, CUT].astype(f32)
            of = G[y, x, CUT].astype(f32)
            fe = jnp.where(top, fl, pltpu.roll(fl, 4, 0))
            for half in range(2):
                oa = jnp.where(top, jnp.broadcast_to(of[2 * half:2 * half + 1], (8, BINS)),
                               jnp.broadcast_to(of[2 * half + 1:2 * half + 2], (8, BINS)))
                pairs[2 * k + half] = fe * oa

    slots([0])

    def two(i, carry):
        slots([2 * i + 1, 2 * i + 2])
        return carry

    lax.fori_loop(0, 8, two, 0)

    last = {}
    for dz, dc in reversed(PEERS):
        to = line(dz, dc)
        c = pltpu.make_async_remote_copy(
            src_ref=stack.at[pl.ds(ROWS * to // 4, 5)], dst_ref=recv.at[slot(-dz, dc)],
            send_sem=s4.at[slot(-dz, dc)], recv_sem=r4.at[slot(-dz, dc)],
            device_id={"tm": to}, device_id_type=pl.DeviceIdType.MESH)
        c.start()
        last[slot(-dz, dc)] = c
    def rows(read):
        pad = jnp.zeros((4, 2 * BINS), f32)
        return jnp.concatenate([read(i).astype(f32) for i in range(5)] + [pad], axis=0).astype(bf16)

    def align(v, shift):
        return pltpu.roll(v, (24 - shift) % 24, 0)[0:ROWS]

    first_row = ROWS * t // 8
    counts = jnp.concatenate([pairs[first_row + i] for i in range(3)], axis=0)
    counts = align(jnp.broadcast_to(jnp.sum(counts, axis=1, keepdims=True), (24, BINS)), ROWS * t % 8)
    gain = jnp.concatenate([(4.0 / math.sqrt(HALF)) / counts] * (LAGS // BINS), axis=1)
    first_row = ROWS * t // 4
    mine = rows(lambda i: stack[first_row + i])
    acc = jnp.dot(mine, tab[t], preferred_element_type=f32)
    for dz, dc in PEERS:
        n = slot(dz, dc)
        last[n].wait_recv()
        lhs = rows(lambda i: recv[n, i])
        acc = acc + jnp.dot(lhs, tab[line(dz, dc)], preferred_element_type=f32)
    out_ref[...] = align(acc, ROWS * t % 4) * gain
    for c in list(first.values()) + sends + list(last.values()):
        c.wait_send()


def per_device(spectra, valid, pair_blocks):
    dma = pltpu.SemaphoreType.DMA
    hbm = pl.BlockSpec(memory_space=pltpu.HBM)
    base, turn = lag_base()
    return pl.pallas_call(
        kernel,
        out_shape=jax.ShapeDtypeStruct((ROWS, LAGS), f32),
        in_specs=[hbm] * 5,
        out_specs=pl.BlockSpec(memory_space=pltpu.VMEM),
        scratch_shapes=[
            pltpu.SMEM((1, SLOTS), jnp.int32),
            pltpu.SMEM((1, 4), jnp.int32),
            pltpu.VMEM((1, 4, 2 * HALF), bf16),
            pltpu.VMEM((2, BINS, LAGS), f32),
            pltpu.VMEM((2, NT, LAGS), f32),
            pltpu.VMEM((NT, 16, BINS), bf16),
            pltpu.VMEM((NT, 16, BINS), bf16),
            pltpu.VMEM((NY, NX, TILES, 8, BINS), bf16),
            pltpu.VMEM((NT, 8, 8, BINS), f32),
            pltpu.VMEM((4 * SLOTS, 4, 2 * BINS), bf16),
            pltpu.VMEM((NT, 5, 4, 2 * BINS), bf16),
            pltpu.VMEM((NT, 2 * BINS, LAGS), bf16),
            pltpu.VMEM((2 * SLOTS, 8, BINS), f32),
            dma((5,)), dma((NT,)), dma((NT,)), dma((8,)), dma((8,)),
            dma((NY, NX)), dma((NY, NX)), dma((NX,)), dma((NX,)),
            dma((8,)), dma((8,)), dma((NT,)), dma((NT,)),
        ],
        compiler_params=pltpu.CompilerParams(
            collective_id=0, has_side_effects=True, vmem_limit_bytes=24 << 20),
    )(*[pltpu.with_memory_space_constraint(a, pltpu.HBM) for a in
        (pair_blocks, valid, spectra, jnp.asarray(base), jnp.asarray(turn))])


def solution(mesh):
    placed = (P("tm", "station", None), P("tm", "station"), P("station", None))
    return jax.shard_map(
        per_device,
        mesh=mesh,
        in_specs=placed,
        out_specs=P(("station", "tm"), None),
        check_vma=False,
    )
```

```python
import math

import jax
import jax.numpy as jnp
import numpy as np
from jax import lax
from jax.experimental import pallas as pl
from jax.experimental.pallas import tpu as pltpu
from jax.sharding import PartitionSpec as P

LAGS = 512
NX, NY = 4, 8
NT = 16
SLOTS = 17
ROWS = 17
HALF = 2048
BINS = HALF // NT
TILES = 17
CUT = 13
DIST = (0, 1, 7, 2, 6, 3, 5, 4)
ORDER = (4, 5, 3, 6, 2, 7, 1, 0)
PEERS = [(dz, dc) for dz in DIST for dc in (0, 1)][1:]
HOP = (1, NY - 1, 2, NY - 2, 1, NY - 1, 2, NY - 2)
f32, bf16 = jnp.float32, jnp.bfloat16


def lag_base():
    shifts = np.arange(LAGS, dtype=np.int64) - LAGS // 2
    unit = math.pi / (2.0 * HALF)

    def both(steps):
        angle = steps[:, None] * shifts[None, :] % (4 * HALF) * unit
        return np.stack([np.cos(angle), np.sin(angle)]).astype(np.float32)

    base = both(2 * np.arange(BINS, dtype=np.int64) + 1)
    turn = both(2 * BINS * np.arange(NT, dtype=np.int64))
    return base, turn


def kernel(plan_ref, valid_ref, spectra_ref, base_ref, turn_ref, out_ref,
           plan, valid, x_ref, base, turn, msg, got, G, own, stack, recv, tab, pairs,
           in_sem, s1, r1, say, ray, sax, rax, sbx, rbx, sby, rby, s4, r4):
    st, t = lax.axis_index("station"), lax.axis_index("tm")
    y, x = st // NX, st % NX
    z, core = t // 2, t % 2

    def line(dz, dc):
        return (z + dz) % 8 * 2 + (core + dc) % 2

    def slot(dz, dc):
        return 2 * DIST.index(dz % 8) + dc

    def tile(n):
        return n if n < CUT else n + 1

    def plane(yy, xx):
        return {"station": (yy % NY) * NX + xx % NX}

    loads = [pltpu.make_async_copy(a, b, in_sem.at[i]) for i, (a, b) in enumerate(
        [(spectra_ref, x_ref), (valid_ref, valid), (plan_ref, plan), (base_ref, base),
         (turn_ref, turn)])]
    for c in loads:
        c.start()

    barrier = pltpu.get_barrier_semaphore()
    for p in reversed(PEERS):
        pl.semaphore_signal(barrier, inc=1, device_id={"tm": line(*p)},
                            device_id_type=pl.DeviceIdType.MESH)
    for j in range(1, NX):
        pl.semaphore_signal(barrier, inc=1, device_id=plane(y, x + j),
                            device_id_type=pl.DeviceIdType.MESH)
    for j in (1, 2, NY - 2, NY - 1):
        pl.semaphore_signal(barrier, inc=1, device_id=plane(y + j, x),
                            device_id_type=pl.DeviceIdType.MESH)

    loads[0].wait()
    loads[1].wait()
    row = lax.broadcasted_iota(jnp.int32, (4, BINS), 0)
    flag = jnp.where(row == 0, valid[0, 0],
                     jnp.where(row == 1, valid[0, 1],
                               jnp.where(row == 2, valid[0, 2], valid[0, 3]))).astype(f32)
    for j in range(NT):
        re = x_ref[0, :, j * BINS:(j + 1) * BINS].astype(f32) * flag
        im = x_ref[0, :, HALF + j * BINS:HALF + (j + 1) * BINS].astype(f32) * flag
        msg[j] = jnp.concatenate([re, im, flag, flag], axis=0).astype(bf16)

    pl.semaphore_wait(barrier, NT - 1 + NX - 1 + 4)

    first = {}
    for dz, dc in reversed(PEERS):
        to = line(dz, dc)
        c = pltpu.make_async_remote_copy(
            src_ref=msg.at[to], dst_ref=got.at[slot(-dz, dc)], send_sem=s1.at[slot(-dz, dc)],
            recv_sem=r1.at[slot(-dz, dc)], device_id={"tm": to},
            device_id_type=pl.DeviceIdType.MESH)
        c.start()
        first[slot(-dz, dc)] = c
    got[0] = msg[t]

    for c in loads[2:]:
        c.wait()

    def fill(j, carry):
        tc = turn[0, pl.ds(j, 1), :]
        ts = turn[1, pl.ds(j, 1), :]
        for i in range(0, BINS, 16):
            bc, bs = base[0, i:i + 16], base[1, i:i + 16]
            tab[j, i:i + 16] = (bc * tc - bs * ts).astype(bf16)
            tab[j, BINS + i:BINS + i + 16] = (-(bs * tc + bc * ts)).astype(bf16)
        return carry

    lax.fori_loop(0, NT, fill, 0)
    sends = []

    def send(ref, to, ssem, rsem):
        c = pltpu.make_async_remote_copy(src_ref=ref, dst_ref=ref, send_sem=ssem, recv_sem=rsem,
                                         device_id=to, device_id_type=pl.DeviceIdType.MESH)
        c.start()
        sends.append(c)
        return c

    def A(yy, xx):
        return G.at[yy % NY, xx % NX, pl.ds(0, CUT)]

    def B(yy, xx):
        return G.at[yy % NY, xx % NX, pl.ds(CUT, TILES - CUT)]

    def BY(yy):
        return G.at[yy % NY, :, pl.ds(CUT, TILES - CUT)]

    def send_ax(n, yy):
        return [send(A(yy, x), plane(y, x + j), sax.at[n, j], rax.at[n, j]) for j in (2, 1, 3)]

    def far(block, n, ssem, rsem):
        return send(block, plane(y + HOP[n], x), ssem.at[n], rsem.at[n])

    def relay(block, half, ssem, rsem):
        return [far(half(y - 2, 0), 6, ssem, rsem), far(half(y + 2, 1), 7, ssem, rsem),
                far(block(y - 2), 4, ssem, rsem), far(block(y + 2), 5, ssem, rsem)]

    def A_half(yy, h):
        return G.at[yy % NY, x, pl.ds(h * (CUT // 2), CUT // 2 if h == 0 else CUT - CUT // 2)]

    def B_half(yy, h):
        n = TILES - CUT
        return G.at[yy % NY, :, pl.ds(CUT + h * (n // 2), n // 2 if h == 0 else n - n // 2)]

    def arrive(n):
        if n > 0:
            first[n].wait_recv()
        G[y, x, tile(n)] = got[n, 0:8]

    for n in range(CUT):
        arrive(n)
    ay = [far(A(y, x), n, say, ray) for n in (2, 3, 0, 1)]
    for n in range(CUT, NT):
        arrive(n)
    lane = lax.broadcasted_iota(jnp.int32, (8, BINS), 1)
    flags = jnp.zeros((8, BINS), f32)
    for n in range(NT):
        flags = jnp.where(lane == n, got[n, 8:16].astype(f32), flags)
    G[y, x, CUT] = flags.astype(bf16)
    bx = [send(B(y, x), plane(y, x + j), sbx.at[j], rbx.at[j]) for j in range(1, NX)]
    ax = send_ax(0, y)
    for n in range(NT):
        mine = got[n, 0:8].astype(f32)
        for q in range(8):
            own[n, q] = jnp.broadcast_to(mine[q:q + 1], (8, BINS))
    for c in bx:
        c.wait_recv()
    by = [far(BY(y), n, sby, rby) for n in (2, 3, 0, 1)]
    ay[0].wait_recv()
    ay[1].wait_recv()
    ay += relay(lambda yy: A(yy, x), A_half, say, ray)
    ay[2].wait_recv()
    ax += send_ax(1, y - 1)
    ay[3].wait_recv()
    ax += send_ax(2, y + 1)
    ax += send_ax(3, y - 2)
    ax += send_ax(4, y + 2)
    by[0].wait_recv()
    by[1].wait_recv()
    by += relay(BY, B_half, sby, rby)
    ay[6].wait_recv()
    ax += send_ax(5, y - 3)
    ay[7].wait_recv()
    ax += send_ax(6, y + 3)
    ay[4].wait_recv()
    ay[5].wait_recv()
    ax += send_ax(7, y + 4)
    for c in by[2:] + ax:
        c.wait_recv()

    top = lax.broadcasted_iota(jnp.int32, (8, BINS), 0) < 4

    def products(zt):
        tiles = []
        for n in range(3):
            blk = plan[0, 2 * zt + n]
            tiles.append((blk // NX, blk % NX))
        acc = [[[None, None] for _ in range(4)] for _ in tiles]
        for h in range(NT):
            g = [G[py, px, tile(h)].astype(f32) for py, px in tiles]
            for a in range(4):
                for c in range(2):
                    o = own[h, 4 * c + a]
                    for n in range(3):
                        p = o * g[n]
                        acc[n][a][c] = p if h == 0 else acc[n][a][c] + p
        for n in range(3):
            for a in range(4):
                p, q = acc[n][a]
                re = p + pltpu.roll(q, 4, 0)
                im = q - pltpu.roll(p, 4, 0)
                stack[zt, 4 * n + a, :, 0:BINS] = re[0:4].astype(bf16)
                stack[zt, 4 * n + a, :, BINS:2 * BINS] = im[0:4].astype(bf16)
        return tiles

    def offset(zt, c):
        return 2 * zt + ROWS * c

    def rows_to(i, dz, dc):
        zt, c = (z + dz) % 8, (core + dc) % 2
        return pltpu.make_async_remote_copy(
            src_ref=stack.at[zt, pl.ds(offset(zt, c) // 4, 5)], dst_ref=recv.at[2 * i + dc],
            send_sem=s4.at[2 * i + dc], recv_sem=r4.at[2 * i + dc],
            device_id={"tm": 2 * zt + c}, device_id_type=pl.DeviceIdType.MESH)

    def give(i, carry):
        dz = 4 + (i + 1) // 2 * (2 * (i % 2) - 1)
        products((z + dz) % 8)
        for dc in (0, 1):
            rows_to(i, dz, dc).start()
        return carry

    lax.fori_loop(0, 7, give, 0)
    tiles = products(z)
    rows_to(7, 0, 1).start()

    of = G[y, x, CUT].astype(f32)
    for n, (py, px) in enumerate(tiles):
        fl = G[py, px, CUT].astype(f32)
        fe = jnp.where(top, fl, pltpu.roll(fl, 4, 0))
        for half in range(2):
            oa = jnp.where(top, jnp.broadcast_to(of[2 * half:2 * half + 1], (8, BINS)),
                           jnp.broadcast_to(of[2 * half + 1:2 * half + 2], (8, BINS)))
            pairs[2 * n + half] = fe * oa

    def rows(read):
        pad = jnp.zeros((4, 2 * BINS), f32)
        return jnp.concatenate([read(i).astype(f32) for i in range(5)] + [pad], axis=0).astype(bf16)

    def align(v, shift):
        return pltpu.roll(v, (24 - shift) % 24, 0)[0:ROWS]

    start = offset(z, core)
    counts = jnp.concatenate([pairs[start // 8 + i] for i in range(3)], axis=0)
    counts = align(jnp.broadcast_to(jnp.sum(counts, axis=1, keepdims=True), (24, BINS)), start % 8)
    gain = jnp.concatenate([(4.0 / math.sqrt(HALF)) / counts] * (LAGS // BINS), axis=1)
    mine = rows(lambda i: stack[z, start // 4 + i])
    acc = jnp.dot(mine, tab[t], preferred_element_type=f32)
    last = []
    for i, dz in reversed(list(enumerate(ORDER))):
        for dc in ((0, 1) if dz else (1,)):
            c = rows_to(i, dz, dc)
            last.append(c)
            c.wait_recv()
            lhs = rows(lambda n: recv[2 * i + dc, n])
            acc = acc + jnp.dot(lhs, tab[line(-dz, dc)], preferred_element_type=f32)
    out_ref[...] = align(acc, start % 4) * gain
    for c in list(first.values()) + sends + last:
        c.wait_send()


def per_device(spectra, valid, pair_blocks):
    dma = pltpu.SemaphoreType.DMA
    hbm = pl.BlockSpec(memory_space=pltpu.HBM)
    base, turn = lag_base()
    return pl.pallas_call(
        kernel,
        out_shape=jax.ShapeDtypeStruct((ROWS, LAGS), f32),
        in_specs=[hbm] * 5,
        out_specs=pl.BlockSpec(memory_space=pltpu.VMEM),
        scratch_shapes=[
            pltpu.SMEM((1, SLOTS), jnp.int32),
            pltpu.SMEM((1, 4), jnp.int32),
            pltpu.VMEM((1, 4, 2 * HALF), bf16),
            pltpu.VMEM((2, BINS, LAGS), f32),
            pltpu.VMEM((2, NT, LAGS), f32),
            pltpu.VMEM((NT, 16, BINS), bf16),
            pltpu.VMEM((NT, 16, BINS), bf16),
            pltpu.VMEM((NY, NX, TILES, 8, BINS), bf16),
            pltpu.VMEM((NT, 8, 8, BINS), f32),
            pltpu.VMEM((8, 12, 4, 2 * BINS), bf16),
            pltpu.VMEM((NT, 5, 4, 2 * BINS), bf16),
            pltpu.VMEM((NT, 2 * BINS, LAGS), bf16),
            pltpu.VMEM((6, 8, BINS), f32),
            dma((5,)), dma((NT,)), dma((NT,)), dma((8,)), dma((8,)),
            dma((NY, NX)), dma((NY, NX)), dma((NX,)), dma((NX,)),
            dma((8,)), dma((8,)), dma((NT,)), dma((NT,)),
        ],
        compiler_params=pltpu.CompilerParams(
            collective_id=0, has_side_effects=True, vmem_limit_bytes=24 << 20),
    )(*[pltpu.with_memory_space_constraint(a, pltpu.HBM) for a in
        (pair_blocks, valid, spectra, jnp.asarray(base), jnp.asarray(turn))])


def solution(mesh):
    placed = (P("tm", "station", None), P("tm", "station"), P("station", None))
    return jax.shard_map(
        per_device,
        mesh=mesh,
        in_specs=placed,
        out_specs=P(("station", "tm"), None),
        check_vma=False,
    )
```

```python
import math

import jax
import jax.numpy as jnp
import numpy as np
from jax import lax
from jax.experimental import pallas as pl
from jax.experimental.pallas import tpu as pltpu
from jax.sharding import PartitionSpec as P

LAGS = 512
NX, NY = 4, 8
NT = 16
SLOTS = 17
ROWS = 17
HALF = 2048
BINS = HALF // NT
TILES = 17
CUT = 11
DIST = (0, 1, 7, 2, 6, 3, 5, 4)
ORDER = (4, 5, 3, 6, 2, 7, 1, 0)
PEERS = [(dz, dc) for dz in DIST for dc in (0, 1)][1:]
HOP = (1, NY - 1, 2, NY - 2, 1, NY - 1, 2, NY - 2)
f32, bf16 = jnp.float32, jnp.bfloat16


def lag_base():
    shifts = np.arange(LAGS, dtype=np.int64) - LAGS // 2
    unit = math.pi / (2.0 * HALF)

    def both(steps):
        angle = steps[:, None] * shifts[None, :] % (4 * HALF) * unit
        return np.stack([np.cos(angle), np.sin(angle)]).astype(np.float32)

    base = both(2 * np.arange(BINS, dtype=np.int64) + 1)
    turn = both(2 * BINS * np.arange(NT, dtype=np.int64))
    return base, turn


def kernel(plan_ref, valid_ref, spectra_ref, base_ref, turn_ref, out_ref,
           plan, valid, x_ref, base, turn, msg, got, G, own, stack, recv, tab, pairs,
           in_sem, s1, r1, say, ray, sax, rax, sbx, rbx, sby, rby, s4, r4):
    st, t = lax.axis_index("station"), lax.axis_index("tm")
    y, x = st // NX, st % NX
    z, core = t // 2, t % 2

    def line(dz, dc):
        return (z + dz) % 8 * 2 + (core + dc) % 2

    def slot(dz, dc):
        return 2 * DIST.index(dz % 8) + dc

    def tile(n):
        return n if n < CUT else n + 1

    def plane(yy, xx):
        return {"station": (yy % NY) * NX + xx % NX}

    loads = [pltpu.make_async_copy(a, b, in_sem.at[i]) for i, (a, b) in enumerate(
        [(spectra_ref, x_ref), (valid_ref, valid), (plan_ref, plan), (base_ref, base),
         (turn_ref, turn)])]
    for c in loads:
        c.start()

    barrier = pltpu.get_barrier_semaphore()
    for p in reversed(PEERS):
        pl.semaphore_signal(barrier, inc=1, device_id={"tm": line(*p)},
                            device_id_type=pl.DeviceIdType.MESH)
    for j in range(1, NX):
        pl.semaphore_signal(barrier, inc=1, device_id=plane(y, x + j),
                            device_id_type=pl.DeviceIdType.MESH)
    for j in (1, 2, 3, 5, 6, 7):
        pl.semaphore_signal(barrier, inc=1, device_id=plane(y + j, x),
                            device_id_type=pl.DeviceIdType.MESH)

    loads[0].wait()
    loads[1].wait()
    row = lax.broadcasted_iota(jnp.int32, (4, BINS), 0)
    flag = jnp.where(row == 0, valid[0, 0],
                     jnp.where(row == 1, valid[0, 1],
                               jnp.where(row == 2, valid[0, 2], valid[0, 3]))).astype(f32)
    for j in range(NT):
        re = x_ref[0, :, j * BINS:(j + 1) * BINS].astype(f32) * flag
        im = x_ref[0, :, HALF + j * BINS:HALF + (j + 1) * BINS].astype(f32) * flag
        msg[j] = jnp.concatenate([re, im, flag, flag], axis=0).astype(bf16)

    pl.semaphore_wait(barrier, NT - 1 + NX - 1 + 6)

    first = {}
    for dz, dc in reversed(PEERS):
        to = line(dz, dc)
        c = pltpu.make_async_remote_copy(
            src_ref=msg.at[to], dst_ref=got.at[slot(-dz, dc)], send_sem=s1.at[slot(-dz, dc)],
            recv_sem=r1.at[slot(-dz, dc)], device_id={"tm": to},
            device_id_type=pl.DeviceIdType.MESH)
        c.start()
        first[slot(-dz, dc)] = c
    got[0] = msg[t]

    for c in loads[2:]:
        c.wait()

    def fill(j, carry):
        tc = turn[0, pl.ds(j, 1), :]
        ts = turn[1, pl.ds(j, 1), :]
        for i in range(0, BINS, 16):
            bc, bs = base[0, i:i + 16], base[1, i:i + 16]
            tab[j, i:i + 16] = (bc * tc - bs * ts).astype(bf16)
            tab[j, BINS + i:BINS + i + 16] = (-(bs * tc + bc * ts)).astype(bf16)
        return carry

    lax.fori_loop(0, NT, fill, 0)
    sends = []

    def send(ref, to, ssem, rsem):
        c = pltpu.make_async_remote_copy(src_ref=ref, dst_ref=ref, send_sem=ssem, recv_sem=rsem,
                                         device_id=to, device_id_type=pl.DeviceIdType.MESH)
        c.start()
        sends.append(c)
        return c

    def A(yy, xx):
        return G.at[yy % NY, xx % NX, pl.ds(0, CUT)]

    def B(yy, xx):
        return G.at[yy % NY, xx % NX, pl.ds(CUT, TILES - CUT)]

    def BY(yy):
        return G.at[yy % NY, :, pl.ds(CUT, TILES - CUT)]

    def send_ax(n, yy):
        return [send(A(yy, x), plane(y, x + j), sax.at[n, j], rax.at[n, j]) for j in (2, 1, 3)]

    def far(block, n, ssem, rsem):
        return send(block, plane(y + HOP[n], x), ssem.at[n], rsem.at[n])

    def relay(block, half, ssem, rsem):
        return [far(half(y - 2, 0), 6, ssem, rsem), far(half(y + 2, 1), 7, ssem, rsem),
                far(block(y - 2), 4, ssem, rsem), far(block(y + 2), 5, ssem, rsem)]

    def A_half(yy, h):
        return G.at[yy % NY, x, pl.ds(h * (CUT // 2), CUT // 2 if h == 0 else CUT - CUT // 2)]

    def B_half(yy, h):
        n = TILES - CUT
        return G.at[yy % NY, :, pl.ds(CUT + h * (n // 2), n // 2 if h == 0 else n - n // 2)]

    def direct(block, ssem, rsem):
        return {j: send(block, plane(y + j, x), ssem.at[j], rsem.at[j]) for j in (3, 5, 2, 6, 1, 7)}

    def fourth(half, ssem, rsem):
        return [send(half(y - 3, 0), plane(y + 1, x), ssem.at[0], rsem.at[0]),
                send(half(y + 3, 1), plane(y - 1, x), ssem.at[4], rsem.at[4])]

    def land(cs):
        for c in cs:
            c.wait_recv()

    def arrive(n):
        if n > 0:
            first[n].wait_recv()
        G[y, x, tile(n)] = got[n, 0:8]

    for n in range(CUT):
        arrive(n)
    ay = direct(A(y, x), say, ray)
    for n in range(CUT, NT):
        arrive(n)
    lane = lax.broadcasted_iota(jnp.int32, (8, BINS), 1)
    flags = jnp.zeros((8, BINS), f32)
    for n in range(NT):
        flags = jnp.where(lane == n, got[n, 8:16].astype(f32), flags)
    G[y, x, CUT] = flags.astype(bf16)
    bx = [send(B(y, x), plane(y, x + j), sbx.at[j], rbx.at[j]) for j in range(1, NX)]
    for n in range(NT):
        mine = got[n, 0:8].astype(f32)
        for q in range(8):
            own[n, q] = jnp.broadcast_to(mine[q:q + 1], (8, BINS))
    for c in bx:
        c.wait_recv()
    by = [far(BY(y), n, sby, rby) for n in (2, 3, 0, 1)]
    ax = send_ax(0, y)
    for n, j in enumerate((1, 7)):
        ay[j].wait_recv()
        ax += send_ax(n + 1, y - j)
    land([ay[3], ay[5]])
    a4 = fourth(A_half, say, ray)
    for n, j in enumerate((3, 5, 2, 6)):
        if n >= 2:
            ay[j].wait_recv()
        ax += send_ax(n + 3, y - j)
    land(by[:2])
    by += relay(BY, B_half, sby, rby)
    land(a4)
    ax += send_ax(7, y + 4)
    land(by[2:] + ax)

    top = lax.broadcasted_iota(jnp.int32, (8, BINS), 0) < 4

    def products(zt):
        tiles = []
        for n in range(3):
            blk = plan[0, 2 * zt + n]
            tiles.append((blk // NX, blk % NX))
        acc = [[[None, None] for _ in range(4)] for _ in tiles]
        for h in range(NT):
            g = [G[py, px, tile(h)].astype(f32) for py, px in tiles]
            for a in range(4):
                for c in range(2):
                    o = own[h, 4 * c + a]
                    for n in range(3):
                        p = o * g[n]
                        acc[n][a][c] = p if h == 0 else acc[n][a][c] + p
        for n in range(3):
            for a in range(4):
                p, q = acc[n][a]
                re = p + pltpu.roll(q, 4, 0)
                im = q - pltpu.roll(p, 4, 0)
                stack[zt, 4 * n + a, :, 0:BINS] = re[0:4].astype(bf16)
                stack[zt, 4 * n + a, :, BINS:2 * BINS] = im[0:4].astype(bf16)
        return tiles

    def offset(zt, c):
        return 2 * zt + ROWS * c

    def rows_to(i, dz, dc):
        zt, c = (z + dz) % 8, (core + dc) % 2
        return pltpu.make_async_remote_copy(
            src_ref=stack.at[zt, pl.ds(offset(zt, c) // 4, 5)], dst_ref=recv.at[2 * i + dc],
            send_sem=s4.at[2 * i + dc], recv_sem=r4.at[2 * i + dc],
            device_id={"tm": 2 * zt + c}, device_id_type=pl.DeviceIdType.MESH)

    def give(i, carry):
        dz = 4 + (i + 1) // 2 * (2 * (i % 2) - 1)
        products((z + dz) % 8)
        for dc in (0, 1):
            rows_to(i, dz, dc).start()
        return carry

    lax.fori_loop(0, 7, give, 0)
    tiles = products(z)
    rows_to(7, 0, 1).start()

    of = G[y, x, CUT].astype(f32)
    for n, (py, px) in enumerate(tiles):
        fl = G[py, px, CUT].astype(f32)
        fe = jnp.where(top, fl, pltpu.roll(fl, 4, 0))
        for half in range(2):
            oa = jnp.where(top, jnp.broadcast_to(of[2 * half:2 * half + 1], (8, BINS)),
                           jnp.broadcast_to(of[2 * half + 1:2 * half + 2], (8, BINS)))
            pairs[2 * n + half] = fe * oa

    def rows(read):
        pad = jnp.zeros((4, 2 * BINS), f32)
        return jnp.concatenate([read(i).astype(f32) for i in range(5)] + [pad], axis=0).astype(bf16)

    def align(v, shift):
        return pltpu.roll(v, (24 - shift) % 24, 0)[0:ROWS]

    start = offset(z, core)
    counts = jnp.concatenate([pairs[start // 8 + i] for i in range(3)], axis=0)
    counts = align(jnp.broadcast_to(jnp.sum(counts, axis=1, keepdims=True), (24, BINS)), start % 8)
    gain = jnp.concatenate([(4.0 / math.sqrt(HALF)) / counts] * (LAGS // BINS), axis=1)
    for c in list(first.values()) + sends:
        c.wait_send()
    mine = rows(lambda i: stack[z, start // 4 + i])
    acc = jnp.dot(mine, tab[t], preferred_element_type=f32)
    last = []
    for i, dz in reversed(list(enumerate(ORDER))):
        for dc in ((0, 1) if dz else (1,)):
            c = rows_to(i, dz, dc)
            last.append(c)
            c.wait_recv()
            lhs = rows(lambda n: recv[2 * i + dc, n])
            acc = acc + jnp.dot(lhs, tab[line(-dz, dc)], preferred_element_type=f32)
    out_ref[...] = align(acc, start % 4) * gain
    for c in last:
        c.wait_send()


def per_device(spectra, valid, pair_blocks):
    dma = pltpu.SemaphoreType.DMA
    hbm = pl.BlockSpec(memory_space=pltpu.HBM)
    base, turn = lag_base()
    return pl.pallas_call(
        kernel,
        out_shape=jax.ShapeDtypeStruct((ROWS, LAGS), f32),
        in_specs=[hbm] * 5,
        out_specs=pl.BlockSpec(memory_space=pltpu.VMEM),
        scratch_shapes=[
            pltpu.SMEM((1, SLOTS), jnp.int32),
            pltpu.SMEM((1, 4), jnp.int32),
            pltpu.VMEM((1, 4, 2 * HALF), bf16),
            pltpu.VMEM((2, BINS, LAGS), f32),
            pltpu.VMEM((2, NT, LAGS), f32),
            pltpu.VMEM((NT, 16, BINS), bf16),
            pltpu.VMEM((NT, 16, BINS), bf16),
            pltpu.VMEM((NY, NX, TILES, 8, BINS), bf16),
            pltpu.VMEM((NT, 8, 8, BINS), f32),
            pltpu.VMEM((8, 12, 4, 2 * BINS), bf16),
            pltpu.VMEM((NT, 5, 4, 2 * BINS), bf16),
            pltpu.VMEM((NT, 2 * BINS, LAGS), bf16),
            pltpu.VMEM((6, 8, BINS), f32),
            dma((5,)), dma((NT,)), dma((NT,)), dma((8,)), dma((8,)),
            dma((NY, NX)), dma((NY, NX)), dma((NX,)), dma((NX,)),
            dma((8,)), dma((8,)), dma((NT,)), dma((NT,)),
        ],
        compiler_params=pltpu.CompilerParams(
            collective_id=0, has_side_effects=True, vmem_limit_bytes=24 << 20),
    )(*[pltpu.with_memory_space_constraint(a, pltpu.HBM) for a in
        (pair_blocks, valid, spectra, jnp.asarray(base), jnp.asarray(turn))])


def solution(mesh):
    placed = (P("tm", "station", None), P("tm", "station"), P("station", None))
    return jax.shard_map(
        per_device,
        mesh=mesh,
        in_specs=placed,
        out_specs=P(("station", "tm"), None),
        check_vma=False,
    )
```

```python
import math

import jax
import jax.numpy as jnp
import numpy as np
from jax import lax
from jax.experimental import pallas as pl
from jax.experimental.pallas import tpu as pltpu
from jax.sharding import PartitionSpec as P

LAGS = 512
NX, NY = 4, 8
NT = 16
SLOTS = 17
ROWS = 17
HALF = 2048
BINS = HALF // NT
TILES = 17
CUT = 11
DIST = (0, 1, 7, 2, 6, 3, 5, 4)
ORDER = (4, 5, 3, 6, 2, 7, 1, 0)
PEERS = [(dz, dc) for dz in DIST for dc in (0, 1)][1:]
f32, bf16 = jnp.float32, jnp.bfloat16


def lag_base():
    shifts = np.arange(LAGS, dtype=np.int64) - LAGS // 2
    unit = math.pi / (2.0 * HALF)

    def both(steps):
        angle = steps[:, None] * shifts[None, :] % (4 * HALF) * unit
        return np.stack([np.cos(angle), np.sin(angle)]).astype(np.float32)

    base = both(2 * np.arange(BINS, dtype=np.int64) + 1)
    turn = both(2 * BINS * np.arange(NT, dtype=np.int64))
    return base, turn


def kernel(plan_ref, valid_ref, spectra_ref, base_ref, turn_ref, out_ref,
           plan, valid, x_ref, base, turn, msg, got, G, own, stack, recv, tab, pairs,
           in_sem, s1, r1, say, ray, sax, rax, sbx, rbx, sby, rby, s4, r4):
    st, t = lax.axis_index("station"), lax.axis_index("tm")
    y, x = st // NX, st % NX
    z, core = t // 2, t % 2

    def line(dz, dc):
        return (z + dz) % 8 * 2 + (core + dc) % 2

    def slot(dz, dc):
        return 2 * DIST.index(dz % 8) + dc

    def tile(n):
        return n if n < CUT else n + 1

    def plane(yy, xx):
        return {"station": (yy % NY) * NX + xx % NX}

    loads = [pltpu.make_async_copy(a, b, in_sem.at[i]) for i, (a, b) in enumerate(
        [(spectra_ref, x_ref), (valid_ref, valid), (plan_ref, plan), (base_ref, base),
         (turn_ref, turn)])]
    for c in loads:
        c.start()

    barrier = pltpu.get_barrier_semaphore()
    for p in reversed(PEERS):
        pl.semaphore_signal(barrier, inc=1, device_id={"tm": line(*p)},
                            device_id_type=pl.DeviceIdType.MESH)
    for j in range(1, NX):
        pl.semaphore_signal(barrier, inc=1, device_id=plane(y, x + j),
                            device_id_type=pl.DeviceIdType.MESH)
    for j in (1, 2, 3, 5, 6, 7):
        pl.semaphore_signal(barrier, inc=1, device_id=plane(y + j, x),
                            device_id_type=pl.DeviceIdType.MESH)

    loads[0].wait()
    loads[1].wait()
    row = lax.broadcasted_iota(jnp.int32, (4, BINS), 0)
    flag = jnp.where(row == 0, valid[0, 0],
                     jnp.where(row == 1, valid[0, 1],
                               jnp.where(row == 2, valid[0, 2], valid[0, 3]))).astype(f32)
    for j in range(NT):
        re = x_ref[0, :, j * BINS:(j + 1) * BINS].astype(f32) * flag
        im = x_ref[0, :, HALF + j * BINS:HALF + (j + 1) * BINS].astype(f32) * flag
        msg[j] = jnp.concatenate([re, im, flag, flag], axis=0).astype(bf16)

    pl.semaphore_wait(barrier, NT - 1 + NX - 1 + 6)

    first = {}
    for dz, dc in reversed(PEERS):
        to = line(dz, dc)
        c = pltpu.make_async_remote_copy(
            src_ref=msg.at[to], dst_ref=got.at[slot(-dz, dc)], send_sem=s1.at[slot(-dz, dc)],
            recv_sem=r1.at[slot(-dz, dc)], device_id={"tm": to},
            device_id_type=pl.DeviceIdType.MESH)
        c.start()
        first[slot(-dz, dc)] = c
    got[0] = msg[t]

    for c in loads[2:]:
        c.wait()

    def fill(j, carry):
        tc = turn[0, pl.ds(j, 1), :]
        ts = turn[1, pl.ds(j, 1), :]
        for i in range(0, BINS, 16):
            bc, bs = base[0, i:i + 16], base[1, i:i + 16]
            tab[j, i:i + 16] = (bc * tc - bs * ts).astype(bf16)
            tab[j, BINS + i:BINS + i + 16] = (-(bs * tc + bc * ts)).astype(bf16)
        return carry

    lax.fori_loop(0, NT, fill, 0)
    sends = []

    def send(src, dst, to, ssem, rsem):
        c = pltpu.make_async_remote_copy(src_ref=src, dst_ref=dst, send_sem=ssem, recv_sem=rsem,
                                         device_id=to, device_id_type=pl.DeviceIdType.MESH)
        c.start()
        sends.append(c)
        return c

    def place(o):
        r = o % NY
        return 2 * r if r < 4 else 15 - 2 * r

    def cut_of(part, half):
        lo, hi = part
        mid = (lo + hi) // 2
        return ((lo, hi), (lo, mid), (mid, hi))[half]

    def A(o, half=0):
        lo, hi = cut_of((0, CUT), half)
        return G.at[place(o), x, pl.ds(lo, hi - lo)]

    def BY(o, half=0):
        lo, hi = cut_of((CUT, TILES), half)
        return G.at[place(o), :, pl.ds(lo, hi - lo)]

    def to_x(p, n, part, sems):
        ref = G.at[pl.ds(p, n), x, pl.ds(part[0], part[1] - part[0])]
        return [send(ref, ref, plane(y, x + j), sems[0].at[p, j], sems[1].at[p, j]) for j in (2, 1, 3)]

    def to_y(block, o, j, n, sems, half=0):
        return send(block(o, half), block(o - j, half), plane(y + j, x), sems[0].at[n], sems[1].at[n])

    def land(cs):
        for c in cs:
            c.wait_recv()

    def arrive(n):
        if n > 0:
            first[n].wait_recv()
        G[0, x, tile(n)] = got[n, 0:8]

    for n in range(CUT):
        arrive(n)
    ay = {j: to_y(A, 0, j, j % NY, (say, ray)) for j in (3, -3, 2, -2, 1, -1)}
    for n in range(CUT, NT):
        arrive(n)
    lane = lax.broadcasted_iota(jnp.int32, (8, BINS), 1)
    flags = jnp.zeros((8, BINS), f32)
    for n in range(NT):
        flags = jnp.where(lane == n, got[n, 8:16].astype(f32), flags)
    G[0, x, CUT] = flags.astype(bf16)
    bx = to_x(0, 1, (CUT, TILES), (sbx, rbx))
    for n in range(NT):
        mine = got[n, 0:8].astype(f32)
        for q in range(8):
            own[n, q] = jnp.broadcast_to(mine[q:q + 1], (8, BINS))
    for c in bx:
        c.wait_recv()
    yb = (sby, rby)
    by = [to_y(BY, 0, j, n, yb) for n, j in enumerate((2, -2, 1, -1))]
    xa = ((0, CUT), (sax, rax))
    ax = to_x(0, 1, *xa)
    land([ay[1], ay[-1]])
    ax += to_x(1, 2, *xa)
    land([ay[3], ay[-3]])
    a4 = [to_y(A, -3, 1, 0, (say, ray), 1), to_y(A, 3, -1, 4, (say, ray), 2)]
    land([ay[2], ay[-2]])
    ax += to_x(3, 2, *xa)
    ax += to_x(5, 2, *xa)
    land(by[:2])
    by += [to_y(BY, -2, 2, 4, yb, 1), to_y(BY, 2, -2, 5, yb, 2),
           to_y(BY, -2, 1, 6, yb), to_y(BY, 2, -1, 7, yb)]
    land(a4)
    ax += to_x(7, 1, *xa)
    land(by[2:] + ax)

    top = lax.broadcasted_iota(jnp.int32, (8, BINS), 0) < 4

    def products(zt):
        tiles = []
        for n in range(3):
            blk = plan[0, 2 * zt + n]
            r = (blk // NX + NY - y) % NY
            tiles.append((jnp.where(r < 4, 2 * r, 15 - 2 * r), blk % NX))
        acc = [[[None, None] for _ in range(4)] for _ in tiles]
        for h in range(NT):
            g = [G[py, px, tile(h)].astype(f32) for py, px in tiles]
            for a in range(4):
                for c in range(2):
                    o = own[h, 4 * c + a]
                    for n in range(3):
                        p = o * g[n]
                        acc[n][a][c] = p if h == 0 else acc[n][a][c] + p
        for n in range(3):
            for a in range(4):
                p, q = acc[n][a]
                re = p + pltpu.roll(q, 4, 0)
                im = q - pltpu.roll(p, 4, 0)
                stack[zt, 4 * n + a, :, 0:BINS] = re[0:4].astype(bf16)
                stack[zt, 4 * n + a, :, BINS:2 * BINS] = im[0:4].astype(bf16)
        return tiles

    def offset(zt, c):
        return 2 * zt + ROWS * c

    def rows_to(i, dz, dc):
        zt, c = (z + dz) % 8, (core + dc) % 2
        return pltpu.make_async_remote_copy(
            src_ref=stack.at[zt, pl.ds(offset(zt, c) // 4, 5)], dst_ref=recv.at[2 * i + dc],
            send_sem=s4.at[2 * i + dc], recv_sem=r4.at[2 * i + dc],
            device_id={"tm": 2 * zt + c}, device_id_type=pl.DeviceIdType.MESH)

    def give(i, carry):
        dz = 4 + (i + 1) // 2 * (2 * (i % 2) - 1)
        products((z + dz) % 8)
        for dc in (0, 1):
            rows_to(i, dz, dc).start()
        return carry

    lax.fori_loop(0, 7, give, 0)
    tiles = products(z)
    rows_to(7, 0, 1).start()

    of = G[0, x, CUT].astype(f32)
    for n, (py, px) in enumerate(tiles):
        fl = G[py, px, CUT].astype(f32)
        fe = jnp.where(top, fl, pltpu.roll(fl, 4, 0))
        for half in range(2):
            oa = jnp.where(top, jnp.broadcast_to(of[2 * half:2 * half + 1], (8, BINS)),
                           jnp.broadcast_to(of[2 * half + 1:2 * half + 2], (8, BINS)))
            pairs[2 * n + half] = fe * oa

    def rows(read):
        pad = jnp.zeros((4, 2 * BINS), f32)
        return jnp.concatenate([read(i).astype(f32) for i in range(5)] + [pad], axis=0).astype(bf16)

    def align(v, shift):
        return pltpu.roll(v, (24 - shift) % 24, 0)[0:ROWS]

    start = offset(z, core)
    counts = jnp.concatenate([pairs[start // 8 + i] for i in range(3)], axis=0)
    counts = align(jnp.broadcast_to(jnp.sum(counts, axis=1, keepdims=True), (24, BINS)), start % 8)
    gain = jnp.concatenate([(4.0 / math.sqrt(HALF)) / counts] * (LAGS // BINS), axis=1)
    for c in list(first.values()) + sends:
        c.wait_send()
    mine = rows(lambda i: stack[z, start // 4 + i])
    acc = jnp.dot(mine, tab[t], preferred_element_type=f32)
    last = []
    for i, dz in reversed(list(enumerate(ORDER))):
        for dc in ((0, 1) if dz else (1,)):
            c = rows_to(i, dz, dc)
            last.append(c)
            c.wait_recv()
            lhs = rows(lambda n: recv[2 * i + dc, n])
            acc = acc + jnp.dot(lhs, tab[line(-dz, dc)], preferred_element_type=f32)
    out_ref[...] = align(acc, start % 4) * gain
    for c in last:
        c.wait_send()


def per_device(spectra, valid, pair_blocks):
    dma = pltpu.SemaphoreType.DMA
    hbm = pl.BlockSpec(memory_space=pltpu.HBM)
    base, turn = lag_base()
    return pl.pallas_call(
        kernel,
        out_shape=jax.ShapeDtypeStruct((ROWS, LAGS), f32),
        in_specs=[hbm] * 5,
        out_specs=pl.BlockSpec(memory_space=pltpu.VMEM),
        scratch_shapes=[
            pltpu.SMEM((1, SLOTS), jnp.int32),
            pltpu.SMEM((1, 4), jnp.int32),
            pltpu.VMEM((1, 4, 2 * HALF), bf16),
            pltpu.VMEM((2, BINS, LAGS), f32),
            pltpu.VMEM((2, NT, LAGS), f32),
            pltpu.VMEM((NT, 16, BINS), bf16),
            pltpu.VMEM((NT, 16, BINS), bf16),
            pltpu.VMEM((NY, NX, TILES, 8, BINS), bf16),
            pltpu.VMEM((NT, 8, 8, BINS), f32),
            pltpu.VMEM((8, 12, 4, 2 * BINS), bf16),
            pltpu.VMEM((NT, 5, 4, 2 * BINS), bf16),
            pltpu.VMEM((NT, 2 * BINS, LAGS), bf16),
            pltpu.VMEM((6, 8, BINS), f32),
            dma((5,)), dma((NT,)), dma((NT,)), dma((8,)), dma((8,)),
            dma((NY, NX)), dma((NY, NX)), dma((1, NX)), dma((1, NX)),
            dma((8,)), dma((8,)), dma((NT,)), dma((NT,)),
        ],
        compiler_params=pltpu.CompilerParams(
            collective_id=0, has_side_effects=True, vmem_limit_bytes=24 << 20),
    )(*[pltpu.with_memory_space_constraint(a, pltpu.HBM) for a in
        (pair_blocks, valid, spectra, jnp.asarray(base), jnp.asarray(turn))])


def solution(mesh):
    placed = (P("tm", "station", None), P("tm", "station"), P("station", None))
    return jax.shard_map(
        per_device,
        mesh=mesh,
        in_specs=placed,
        out_specs=P(("station", "tm"), None),
        check_vma=False,
    )
```

```python
import math

import jax
import jax.numpy as jnp
import numpy as np
from jax import lax
from jax.experimental import pallas as pl
from jax.experimental.pallas import tpu as pltpu
from jax.sharding import PartitionSpec as P

LAGS = 512
NX, NY = 4, 8
NT = 16
SLOTS = 17
ROWS = 17
HALF = 2048
BINS = HALF // NT
TILES = 17
CUT = 13
DIST = (0, 1, 7, 2, 6, 3, 5, 4)
ORDER = (4, 5, 3, 6, 2, 7, 1, 0)
PEERS = [(dz, dc) for dz in DIST for dc in (0, 1)][1:]
HOP = (1, NY - 1, 2, NY - 2, 1, NY - 1, 2, NY - 2)
f32, bf16 = jnp.float32, jnp.bfloat16


def lag_base():
    shifts = np.arange(LAGS, dtype=np.int64) - LAGS // 2
    unit = math.pi / (2.0 * HALF)

    def both(steps):
        angle = steps[:, None] * shifts[None, :] % (4 * HALF) * unit
        return np.stack([np.cos(angle), np.sin(angle)]).astype(np.float32)

    base = both(2 * np.arange(BINS, dtype=np.int64) + 1)
    turn = both(2 * BINS * np.arange(NT, dtype=np.int64))
    return base, turn


def kernel(plan_ref, valid_ref, spectra_ref, base_ref, turn_ref, out_ref,
           plan, valid, x_ref, base, turn, msg, got, G, own, stack, recv, tab, pairs,
           in_sem, s1, r1, say, ray, sax, rax, sbx, rbx, sby, rby, s4, r4):
    st, t = lax.axis_index("station"), lax.axis_index("tm")
    y, x = st // NX, st % NX
    z, core = t // 2, t % 2

    def line(dz, dc):
        return (z + dz) % 8 * 2 + (core + dc) % 2

    def slot(dz, dc):
        return 2 * DIST.index(dz % 8) + dc

    def tile(n):
        return n if n < CUT else n + 1

    def plane(yy, xx):
        return {"station": (yy % NY) * NX + xx % NX}

    loads = [pltpu.make_async_copy(a, b, in_sem.at[i]) for i, (a, b) in enumerate(
        [(spectra_ref, x_ref), (valid_ref, valid), (plan_ref, plan), (base_ref, base),
         (turn_ref, turn)])]
    for c in loads:
        c.start()

    barrier = pltpu.get_barrier_semaphore()
    for p in reversed(PEERS):
        pl.semaphore_signal(barrier, inc=1, device_id={"tm": line(*p)},
                            device_id_type=pl.DeviceIdType.MESH)
    for j in range(1, NX):
        pl.semaphore_signal(barrier, inc=1, device_id=plane(y, x + j),
                            device_id_type=pl.DeviceIdType.MESH)
    for j in (1, 2, NY - 2, NY - 1):
        pl.semaphore_signal(barrier, inc=1, device_id=plane(y + j, x),
                            device_id_type=pl.DeviceIdType.MESH)

    loads[0].wait()
    loads[1].wait()
    row = lax.broadcasted_iota(jnp.int32, (4, BINS), 0)
    flag = jnp.where(row == 0, valid[0, 0],
                     jnp.where(row == 1, valid[0, 1],
                               jnp.where(row == 2, valid[0, 2], valid[0, 3]))).astype(f32)
    for j in range(NT):
        re = x_ref[0, :, j * BINS:(j + 1) * BINS].astype(f32) * flag
        im = x_ref[0, :, HALF + j * BINS:HALF + (j + 1) * BINS].astype(f32) * flag
        msg[j] = jnp.concatenate([re, im, flag, flag], axis=0).astype(bf16)

    pl.semaphore_wait(barrier, NT - 1 + NX - 1 + 4)

    first = {}
    for dz, dc in reversed(PEERS):
        to = line(dz, dc)
        c = pltpu.make_async_remote_copy(
            src_ref=msg.at[to], dst_ref=got.at[slot(-dz, dc)], send_sem=s1.at[slot(-dz, dc)],
            recv_sem=r1.at[slot(-dz, dc)], device_id={"tm": to},
            device_id_type=pl.DeviceIdType.MESH)
        c.start()
        first[slot(-dz, dc)] = c
    got[0] = msg[t]

    for c in loads[2:]:
        c.wait()

    def fill(j, carry):
        tc = turn[0, pl.ds(j, 1), :]
        ts = turn[1, pl.ds(j, 1), :]
        for i in range(0, BINS, 16):
            bc, bs = base[0, i:i + 16], base[1, i:i + 16]
            tab[j, i:i + 16] = (bc * tc - bs * ts).astype(bf16)
            tab[j, BINS + i:BINS + i + 16] = (-(bs * tc + bc * ts)).astype(bf16)
        return carry

    lax.fori_loop(0, NT, fill, 0)
    sends = []

    def send(ref, to, ssem, rsem):
        c = pltpu.make_async_remote_copy(src_ref=ref, dst_ref=ref, send_sem=ssem, recv_sem=rsem,
                                         device_id=to, device_id_type=pl.DeviceIdType.MESH)
        c.start()
        sends.append(c)
        return c

    def A(yy, xx):
        return G.at[yy % NY, xx % NX, pl.ds(0, CUT)]

    def B(yy, xx):
        return G.at[yy % NY, xx % NX, pl.ds(CUT, TILES - CUT)]

    def BY(yy):
        return G.at[yy % NY, :, pl.ds(CUT, TILES - CUT)]

    def send_ax(n, yy):
        return [send(A(yy, x), plane(y, x + j), sax.at[n, j], rax.at[n, j]) for j in (2, 1, 3)]

    def far(block, n, ssem, rsem):
        return send(block, plane(y + HOP[n], x), ssem.at[n], rsem.at[n])

    def relay(block, half, ssem, rsem):
        return [far(half(y - 2, 0), 6, ssem, rsem), far(half(y + 2, 1), 7, ssem, rsem),
                far(block(y - 2), 4, ssem, rsem), far(block(y + 2), 5, ssem, rsem)]

    def A_half(yy, h):
        return G.at[yy % NY, x, pl.ds(h * (CUT // 2), CUT // 2 if h == 0 else CUT - CUT // 2)]

    def B_half(yy, h):
        n = TILES - CUT
        return G.at[yy % NY, :, pl.ds(CUT + h * (n // 2), n // 2 if h == 0 else n - n // 2)]

    def arrive(n):
        if n > 0:
            first[n].wait_recv()
        G[y, x, tile(n)] = got[n, 0:8]

    for n in range(CUT):
        arrive(n)
    ay = [far(A(y, x), n, say, ray) for n in (2, 3, 0, 1)]
    for n in range(CUT, NT):
        arrive(n)
    lane = lax.broadcasted_iota(jnp.int32, (8, BINS), 1)
    flags = jnp.zeros((8, BINS), f32)
    for n in range(NT):
        flags = jnp.where(lane == n, got[n, 8:16].astype(f32), flags)
    G[y, x, CUT] = flags.astype(bf16)
    bx = [send(B(y, x), plane(y, x + j), sbx.at[j], rbx.at[j]) for j in range(1, NX)]
    for n in range(NT):
        mine = got[n, 0:8].astype(f32)
        for q in range(8):
            own[n, q] = jnp.broadcast_to(mine[q:q + 1], (8, BINS))
    for c in bx:
        c.wait_recv()
    by = [far(BY(y), n, sby, rby) for n in (2, 3, 0, 1)]
    ax = send_ax(0, y)
    ay[0].wait_recv()
    ay[1].wait_recv()
    ay += relay(lambda yy: A(yy, x), A_half, say, ray)
    ay[2].wait_recv()
    ax += send_ax(1, y - 1)
    ay[3].wait_recv()
    ax += send_ax(2, y + 1)
    ax += send_ax(3, y - 2)
    ax += send_ax(4, y + 2)
    by[0].wait_recv()
    by[1].wait_recv()
    by += relay(BY, B_half, sby, rby)
    ay[6].wait_recv()
    ax += send_ax(5, y - 3)
    ay[7].wait_recv()
    ax += send_ax(6, y + 3)
    ay[4].wait_recv()
    ay[5].wait_recv()
    ax += send_ax(7, y + 4)
    for c in by[2:] + ax:
        c.wait_recv()

    top = lax.broadcasted_iota(jnp.int32, (8, BINS), 0) < 4

    def products(zt):
        tiles = []
        for n in range(3):
            blk = plan[0, 2 * zt + n]
            tiles.append((blk // NX, blk % NX))
        acc = [[[None, None] for _ in range(4)] for _ in tiles]
        for h in range(NT):
            g = [G[py, px, tile(h)].astype(f32) for py, px in tiles]
            for a in range(4):
                for c in range(2):
                    o = own[h, 4 * c + a]
                    for n in range(3):
                        p = o * g[n]
                        acc[n][a][c] = p if h == 0 else acc[n][a][c] + p
        for n in range(3):
            for a in range(4):
                p, q = acc[n][a]
                re = p + pltpu.roll(q, 4, 0)
                im = q - pltpu.roll(p, 4, 0)
                stack[zt, 4 * n + a, :, 0:BINS] = re[0:4].astype(bf16)
                stack[zt, 4 * n + a, :, BINS:2 * BINS] = im[0:4].astype(bf16)
        return tiles

    def offset(zt, c):
        return 2 * zt + ROWS * c

    def rows_to(i, dz, dc):
        zt, c = (z + dz) % 8, (core + dc) % 2
        return pltpu.make_async_remote_copy(
            src_ref=stack.at[zt, pl.ds(offset(zt, c) // 4, 5)], dst_ref=recv.at[2 * i + dc],
            send_sem=s4.at[2 * i + dc], recv_sem=r4.at[2 * i + dc],
            device_id={"tm": 2 * zt + c}, device_id_type=pl.DeviceIdType.MESH)

    def give(i, carry):
        dz = 4 + (i + 1) // 2 * (2 * (i % 2) - 1)
        products((z + dz) % 8)
        for dc in (0, 1):
            rows_to(i, dz, dc).start()
        return carry

    lax.fori_loop(0, 7, give, 0)
    tiles = products(z)
    rows_to(7, 0, 1).start()

    of = G[y, x, CUT].astype(f32)
    for n, (py, px) in enumerate(tiles):
        fl = G[py, px, CUT].astype(f32)
        fe = jnp.where(top, fl, pltpu.roll(fl, 4, 0))
        for half in range(2):
            oa = jnp.where(top, jnp.broadcast_to(of[2 * half:2 * half + 1], (8, BINS)),
                           jnp.broadcast_to(of[2 * half + 1:2 * half + 2], (8, BINS)))
            pairs[2 * n + half] = fe * oa

    def rows(read):
        pad = jnp.zeros((4, 2 * BINS), f32)
        return jnp.concatenate([read(i).astype(f32) for i in range(5)] + [pad], axis=0).astype(bf16)

    def align(v, shift):
        return pltpu.roll(v, (24 - shift) % 24, 0)[0:ROWS]

    start = offset(z, core)
    counts = jnp.concatenate([pairs[start // 8 + i] for i in range(3)], axis=0)
    counts = align(jnp.broadcast_to(jnp.sum(counts, axis=1, keepdims=True), (24, BINS)), start % 8)
    gain = jnp.concatenate([(4.0 / math.sqrt(HALF)) / counts] * (LAGS // BINS), axis=1)
    for c in list(first.values()) + sends:
        c.wait_send()
    mine = rows(lambda i: stack[z, start // 4 + i])
    acc = jnp.dot(mine, tab[t], preferred_element_type=f32)
    last = []
    for i, dz in reversed(list(enumerate(ORDER))):
        for dc in ((0, 1) if dz else (1,)):
            c = rows_to(i, dz, dc)
            last.append(c)
            c.wait_recv()
            lhs = rows(lambda n: recv[2 * i + dc, n])
            acc = acc + jnp.dot(lhs, tab[line(-dz, dc)], preferred_element_type=f32)
    out_ref[...] = align(acc, start % 4) * gain
    for c in last:
        c.wait_send()


def per_device(spectra, valid, pair_blocks):
    dma = pltpu.SemaphoreType.DMA
    hbm = pl.BlockSpec(memory_space=pltpu.HBM)
    base, turn = lag_base()
    return pl.pallas_call(
        kernel,
        out_shape=jax.ShapeDtypeStruct((ROWS, LAGS), f32),
        in_specs=[hbm] * 5,
        out_specs=pl.BlockSpec(memory_space=pltpu.VMEM),
        scratch_shapes=[
            pltpu.SMEM((1, SLOTS), jnp.int32),
            pltpu.SMEM((1, 4), jnp.int32),
            pltpu.VMEM((1, 4, 2 * HALF), bf16),
            pltpu.VMEM((2, BINS, LAGS), f32),
            pltpu.VMEM((2, NT, LAGS), f32),
            pltpu.VMEM((NT, 16, BINS), bf16),
            pltpu.VMEM((NT, 16, BINS), bf16),
            pltpu.VMEM((NY, NX, TILES, 8, BINS), bf16),
            pltpu.VMEM((NT, 8, 8, BINS), f32),
            pltpu.VMEM((8, 12, 4, 2 * BINS), bf16),
            pltpu.VMEM((NT, 5, 4, 2 * BINS), bf16),
            pltpu.VMEM((NT, 2 * BINS, LAGS), bf16),
            pltpu.VMEM((6, 8, BINS), f32),
            dma((5,)), dma((NT,)), dma((NT,)), dma((8,)), dma((8,)),
            dma((NY, NX)), dma((NY, NX)), dma((NX,)), dma((NX,)),
            dma((8,)), dma((8,)), dma((NT,)), dma((NT,)),
        ],
        compiler_params=pltpu.CompilerParams(
            collective_id=0, has_side_effects=True, vmem_limit_bytes=24 << 20),
    )(*[pltpu.with_memory_space_constraint(a, pltpu.HBM) for a in
        (pair_blocks, valid, spectra, jnp.asarray(base), jnp.asarray(turn))])


def solution(mesh):
    placed = (P("tm", "station", None), P("tm", "station"), P("station", None))
    return jax.shard_map(
        per_device,
        mesh=mesh,
        in_specs=placed,
        out_specs=P(("station", "tm"), None),
        check_vma=False,
    )
```
